32 devices in a mesh: groups: 2 (over y), rows: 4 (over z), cols: 4 (over x, core).
Axes of the slice: x: 2, y: 2, z: 4, core: 2. Of those that a mesh axis runs over, the one named last changes fastest.
Arguments:
- coupling: bfloat16 [6, 8192, 8192], P('groups', 'cols', 'rows'), parts along dimension 0, may hold values from -0.0625 to 0.0625
- diag_inverse: bfloat16 [6, 8192, 8192], P('groups', 'rows', 'cols'), parts along dimension 0, as said below
- loads: bfloat16 [6, 128, 8192], P('groups', None, 'cols'), parts along dimension 0, may hold values from -6 to 6
- axle_index: int32 [64], P('groups'), parts along dimension 0, may hold values from 0 to 127
Outputs:
- influence: float32 [6, 32, 8192], P('groups', None, 'cols'), parts along dimension 0
- forward: float32 [6, 32, 8192], P('groups', None, 'rows'), parts along dimension 0
The draws below stay inside these ranges and needn't reach their ends.
There are 2 independent parts, one for each index of `groups`. The reference program is written for one: setup_inputs(seed, part) draws one part's arguments, and reference() takes and returns one part's arrays. A program takes and returns all parts, laid end to end along the dimension named above; each array names one. Nothing has to cross between parts.
Inputs may be any that keep to these rules, and one draw needn't show every extreme that they name: `diag_inverse`: lower triangular with a positive diagonal.
All inputs are finite; a program needn't handle non-finite values.
Results may differ from the reference program's by a relative error of at most 0.0065.
Values sent between devices are 32-bit elements; how exact they have to be, the bound alone decides.
No kernel may reach another device: no remote copies, remote signals or barrier semaphores. Data moves between devices by JAX's collectives and lax.ppermute only.
A program may use at most 128 MiB of HBM per device.

```python
import jax
import jax.numpy as jnp

S = 8192
LEVELS = 3
PAIRS = 3
LOADS = 32
POSITIONS = 128


def draw_diag_inverse(key, part):
    key_diag = jax.random.fold_in(key, 11)
    key_off = jax.random.fold_in(key, 23)
    diag = jnp.exp(jax.random.uniform(key_diag, (LEVELS, S), jnp.float32, jnp.log(0.5), jnp.log(2.0)))
    off = jax.random.normal(key_off, (LEVELS, S, S), jnp.float32) * (0.6 / S ** 0.5)
    row_ids = jnp.arange(S)[:, None]
    col_ids = jnp.arange(S)[None, :]
    lower = jnp.where(row_ids > col_ids, off, 0.0)
    eye = (row_ids == col_ids).astype(jnp.float32)
    return (lower + eye[None] * diag[:, :, None]).astype(jnp.bfloat16)


def set_ends(entries, key, smallest, largest):
    spot = [jax.random.randint(jax.random.fold_in(key, axis), (), 0, length) for axis, length in enumerate(entries.shape)]
    longest = entries.shape.index(max(entries.shape))
    next_to = spot[:longest] + [(spot[longest] + 1) % entries.shape[longest]] + spot[longest + 1:]
    return entries.at[tuple(spot)].set(smallest).at[tuple(next_to)].set(largest)


def spiked(result, rng, source, target, parts, factor):
    def block_of(axis_at):
        return (jnp.arange(result.shape[axis_at]) // (result.shape[axis_at] // parts)).reshape((-1,) + (1,) * (result.ndim - 1 - axis_at))

    first = jax.random.permutation(rng, parts)[block_of(target)]
    other_side = (block_of(target) + parts // 2) % parts
    return jnp.where((block_of(source) == first) | (block_of(source) == other_side), factor * result, result)


def levels(own_key, shape, pieces, smallest, top_value):
    loudness = 1.0
    for axis_at, shards_of in pieces:
        draws = jax.random.uniform(jax.random.fold_in(jax.random.fold_in(own_key, 6), axis_at), (shards_of,), jnp.float32, smallest / len(pieces), top_value / len(pieces))
        loudness = loudness * jnp.repeat(jnp.exp(draws), shape[axis_at] // shards_of).reshape((-1,) + (1,) * (len(shape) - 1 - axis_at))
    return loudness


def bell_draw(stream_key, extent, width, most, pieces=(), held_as=jnp.bfloat16):
    drawn = width * jax.random.normal(stream_key, extent, jnp.float32)
    if pieces:
        drawn = drawn * levels(stream_key, extent, pieces, -0.22, 0.18)
    return jnp.clip(drawn, -most, most).astype(held_as)


def heavy_noise(key, dims, spread, bound, split, heavy, held_as=jnp.bfloat16):
    values = spread * jax.random.normal(key, dims, jnp.float32)
    if split:
        values = values * levels(key, dims, split, -0.22, 0.18)
    return jnp.clip(spiked(values, jax.random.fold_in(key, 3), *heavy), -bound, bound).astype(held_as)


def setup_inputs(seed: int = 0, part: int = 0) -> dict:
    keys = jax.random.split(jax.random.key(seed), 5)
    part_splits = jax.random.split(jax.random.fold_in(keys[4], part), 5)
    coupling = heavy_noise(part_splits[0], (PAIRS, S, S), (2 * S) ** -0.5, 0.0625, ((1, 4), (2, 4)), (2, 1, 4, 2.0))
    diag_inverse = draw_diag_inverse(jax.random.fold_in(jax.random.fold_in(keys[4], part), 71), part)
    loads = bell_draw(part_splits[2], (LEVELS, POSITIONS, S), 1.0, 6.0, ((2, 4),))
    axle_index = set_ends(jax.random.randint(part_splits[3], (LOADS,), 0, POSITIONS), jax.random.fold_in(part_splits[3], 1), 0, POSITIONS - 1).astype(jnp.int32)
    return dict(coupling=coupling, diag_inverse=diag_inverse, loads=loads, axle_index=axle_index)


def pair_index(high, low):
    return high * (high - 1) // 2 + low


def reference(coupling, diag_inverse, loads, axle_index):
    rhs = loads[:, axle_index, :].astype(jnp.float32)
    solved = []
    for level in range(LEVELS):
        resid = rhs[level]
        for lower in range(level):
            resid = resid - jnp.dot(solved[lower].astype(jnp.bfloat16), coupling[pair_index(level, lower)].T, preferred_element_type=jnp.float32)
        solved.append(jnp.dot(resid.astype(jnp.bfloat16), diag_inverse[level].T, preferred_element_type=jnp.float32))
    answers = [None] * LEVELS
    for level in range(LEVELS - 1, -1, -1):
        resid = solved[level]
        for upper in range(level + 1, LEVELS):
            resid = resid - jnp.dot(answers[upper].astype(jnp.bfloat16), coupling[pair_index(upper, level)], preferred_element_type=jnp.float32)
        answers[level] = jnp.dot(resid.astype(jnp.bfloat16), diag_inverse[level], preferred_element_type=jnp.float32)
    return jnp.stack(answers), jnp.stack(solved)
```

```python
import jax
import jax.numpy as jnp
from jax import lax
from jax.sharding import PartitionSpec as P

LEVELS = 3
DIRECT_MAX = 8


def pair_index(high, low):
    return high * (high - 1) // 2 + low


def swap(value, axis, size, step):
    return lax.ppermute(value, axis, [(i, i ^ step) for i in range(size)])


def sum_direct(value, axis, size):
    me = lax.axis_index(axis)
    width = value.shape[1] // size

    def chunk(step):
        return lax.dynamic_slice_in_dim(value, (me ^ step) * width, width, axis=1)

    got = [swap(chunk(step), axis, size, step) for step in range(1, size)]
    total = chunk(0)
    for piece in got:
        total = total + piece
    out = lax.dynamic_update_slice_in_dim(jnp.zeros_like(value), total, me * width, axis=1)
    for step in range(1, size):
        out = lax.dynamic_update_slice_in_dim(
            out, swap(total, axis, size, step), (me ^ step) * width, axis=1
        )
    return out


def sum_halves(value, axis, size):
    if size == 1:
        return value
    me = lax.axis_index(axis)
    odd = me % 2 == 1
    half = value.shape[1] // 2
    low, high = value[:, :half], value[:, half:]
    kept = jnp.where(odd, high, low) + swap(jnp.where(odd, low, high), axis, size, 1)
    step = 2
    while step < size:
        kept = kept + swap(kept, axis, size, step)
        step *= 2
    other = swap(kept, axis, size, 1)
    return jnp.concatenate([jnp.where(odd, other, kept), jnp.where(odd, kept, other)], axis=1)


def power_of_two(size):
    return size & (size - 1) == 0


def lower_term(vector_bf, block):
    return jnp.einsum("lj,ij->li", vector_bf, block, preferred_element_type=jnp.float32)


def upper_term(vector_bf, block):
    return jnp.einsum("li,ij->lj", vector_bf, block, preferred_element_type=jnp.float32)


def body(coupling, diag_inverse, loads, axle_index, *, n_rows, n_cols):
    def over_rows(value):
        if power_of_two(n_rows) and n_rows <= DIRECT_MAX:
            return sum_direct(value, "rows", n_rows)
        return lax.psum(value, "rows")

    def over_cols(value):
        if power_of_two(n_cols):
            return sum_halves(value, "cols", n_cols)
        return lax.psum(value, "cols")

    positions = loads.shape[1]
    selector = (axle_index[:, None] == jnp.arange(positions, dtype=jnp.int32)[None, :]).astype(
        jnp.bfloat16
    )
    rhs = jnp.einsum("lp,kpc->klc", selector, loads, preferred_element_type=jnp.float32)
    solved = []
    solved_bf = []
    for level in range(LEVELS):
        resid = rhs[level]
        if level > 0:
            partial_value = lower_term(solved_bf[0], coupling[pair_index(level, 0)])
            for lower in range(1, level):
                partial_value = partial_value + lower_term(
                    solved_bf[lower], coupling[pair_index(level, lower)]
                )
            resid = resid - over_rows(partial_value)
        value = over_cols(lower_term(resid.astype(jnp.bfloat16), diag_inverse[level]))
        solved.append(value)
        solved_bf.append(value.astype(jnp.bfloat16))
    answers = [None] * LEVELS
    answers_bf = [None] * LEVELS
    for level in range(LEVELS - 1, -1, -1):
        resid = solved[level]
        if level < LEVELS - 1:
            partial_value = upper_term(
                answers_bf[LEVELS - 1], coupling[pair_index(LEVELS - 1, level)]
            )
            for upper in range(level + 1, LEVELS - 1):
                partial_value = partial_value + upper_term(
                    answers_bf[upper], coupling[pair_index(upper, level)]
                )
            resid = resid - over_cols(partial_value)
        value = over_rows(upper_term(resid.astype(jnp.bfloat16), diag_inverse[level]))
        answers[level] = value
        answers_bf[level] = value.astype(jnp.bfloat16)
    return jnp.stack(answers), jnp.stack(solved)


def solution(mesh):
    placed = (
        P("groups", "cols", "rows"),
        P("groups", "rows", "cols"),
        P("groups", None, "cols"),
        P("groups"),
    )

    def local(coupling, diag_inverse, loads, axle_index):
        return body(
            coupling,
            diag_inverse,
            loads,
            axle_index,
            n_rows=mesh.shape["rows"],
            n_cols=mesh.shape["cols"],
        )

    return jax.shard_map(
        local,
        mesh=mesh,
        in_specs=placed,
        out_specs=(P("groups", None, "cols"), P("groups", None, "rows")),
        check_vma=False,
    )
```

```python
import functools
import jax
import jax.numpy as jnp
from jax import lax
from jax.experimental import pallas as pl
from jax.experimental.pallas import tpu as pltpu
from jax.sharding import PartitionSpec as P

LEVELS = 3
STREAMS = 2
COPIES = 8
IN_VMEM = pl.BlockSpec(memory_space=pltpu.VMEM)
IN_PLACE = pl.BlockSpec(memory_space=pltpu.HBM)
LOWER = (((1,), (1,)), ((), ()))
UPPER = (((1,), (0,)), ((), ()))


def pair_index(high, low):
    return high * (high - 1) // 2 + low


def params():
    return pltpu.CompilerParams(vmem_limit_bytes=2 << 20)


def block_copies(blocks_ref, out_ref, sems, index):
    height = out_ref.shape[0] // COPIES
    return [
        pltpu.make_async_copy(
            blocks_ref.at[index, pl.ds(i * height, height), :],
            out_ref.at[pl.ds(i * height, height), :],
            sems.at[i],
        )
        for i in range(COPIES)
    ]


def fetch(blocks, index):
    def kernel(blocks_ref, out_ref, sems):
        copies = block_copies(blocks_ref, out_ref, sems, index)
        for copy in copies:
            copy.start()
        for copy in copies:
            copy.wait()

    return pl.pallas_call(
        kernel,
        out_shape=jax.ShapeDtypeStruct(blocks.shape[1:], blocks.dtype),
        in_specs=[IN_PLACE],
        out_specs=IN_VMEM,
        scratch_shapes=[pltpu.SemaphoreType.DMA((COPIES,))],
        compiler_params=params(),
        name="fetch",
    )(pltpu.with_memory_space_constraint(blocks, pltpu.HBM))


def fetch_and_apply(vector, blocks, index):
    rows, cols = blocks.shape[1:]
    height = rows // COPIES

    def kernel(vector_ref, blocks_ref, block_ref, out_ref, sems):
        copies = block_copies(blocks_ref, block_ref, sems, index)
        for copy in copies:
            copy.start()
        vector_bf = vector_ref[...].astype(jnp.bfloat16)
        for i, copy in enumerate(copies):
            copy.wait()
            span = pl.ds(i * height, height)
            out_ref[:, span] = lax.dot_general(
                vector_bf, block_ref[span, :], LOWER, preferred_element_type=jnp.float32
            )

    return pl.pallas_call(
        kernel,
        out_shape=(
            jax.ShapeDtypeStruct((rows, cols), blocks.dtype),
            jax.ShapeDtypeStruct((vector.shape[0], rows), jnp.float32),
        ),
        in_specs=[IN_VMEM, IN_PLACE],
        out_specs=(IN_VMEM, IN_VMEM),
        scratch_shapes=[pltpu.SemaphoreType.DMA((COPIES,))],
        compiler_params=params(),
        name="fetch_and_apply",
    )(vector, pltpu.with_memory_space_constraint(blocks, pltpu.HBM))


def apply(vector, block, dims):
    width = block.shape[0] if dims is LOWER else block.shape[1]

    def kernel(vector_ref, block_ref, out_ref):
        out_ref[...] = lax.dot_general(
            vector_ref[...].astype(jnp.bfloat16),
            block_ref[...],
            dims,
            preferred_element_type=jnp.float32,
        )

    return pl.pallas_call(
        kernel,
        out_shape=jax.ShapeDtypeStruct((vector.shape[0], width), jnp.float32),
        in_specs=[IN_VMEM, IN_VMEM],
        out_specs=IN_VMEM,
        compiler_params=params(),
        name="apply_lower" if dims is LOWER else "apply_upper",
    )(vector, block)


class Order:
    def __init__(self, first):
        self.last = first

    def after(self, *values):
        *values, self.last = lax.optimization_barrier((*values, self.last))
        return values

    def run(self, function, *values):
        result = function(*self.after(*values))
        self.last = result
        return result


def body(coupling, diag_inverse, loads, axle_index, *, sizes):
    positions = loads.shape[1]
    selector = (axle_index[:, None] == jnp.arange(positions, dtype=jnp.int32)[None, :]).astype(
        jnp.bfloat16
    )
    rhs = jnp.einsum("lp,kpc->klc", selector, loads, preferred_element_type=jnp.float32)
    count = rhs.shape[1] // STREAMS
    order = Order(rhs)
    blocks = {}
    solved = {}
    answers = {}
    early = {}

    def bring(kind, index):
        if (kind, index) not in blocks:
            source = diag_inverse if kind == "diag" else coupling
            blocks[kind, index] = order.run(lambda a: fetch(a, index), source)

    def all_sum(value, axis):
        size = sizes[axis]
        step = 1
        while step < size:
            (value,) = order.after(value)
            other = lax.ppermute(value, axis, [(i, i ^ step) for i in range(size)])
            yield
            value = order.run(jnp.add, value, other)
            step *= 2
        return value

    def times(vector, kind, index, dims):
        bring(kind, index)
        return order.run(lambda a, b: apply(a, b, dims), vector, blocks[kind, index])

    def far_term(high, low, me, found, dims):
        if (high, low, me, dims) not in early:
            source = low if dims is LOWER else high
            early[high, low, me, dims] = times(
                found[source, me], "coupling", pair_index(high, low), dims
            )
        return early[high, low, me, dims]

    def stream(me, first):
        part = first
        for level in range(LEVELS):
            if level > 0:
                part = times(solved[level - 1, me], "coupling", pair_index(level, level - 1), LOWER)
                for lower in range(level - 1):
                    part = part + far_term(level, lower, me, solved, LOWER)
                total = yield from all_sum(part, "rows")
                resid = rhs[level, me * count : (me + 1) * count] - total
                part = times(resid, "diag", level, LOWER)
            yield
            solved[level, me] = yield from all_sum(part, "cols")
        for level in range(LEVELS - 1, -1, -1):
            resid = solved[level, me]
            if level < LEVELS - 1:
                part = times(answers[level + 1, me], "coupling", pair_index(level + 1, level), UPPER)
                for upper in range(level + 2, LEVELS):
                    part = part + far_term(upper, level, me, answers, UPPER)
                resid = resid - (yield from all_sum(part, "cols"))
            part = times(resid, "diag", level, UPPER)
            answers[level, me] = yield from all_sum(part, "rows")

    block, first = fetch_and_apply(rhs[0], diag_inverse, 0)
    blocks["diag", 0] = block
    order.last = first
    lanes = [stream(me, first[me * count : (me + 1) * count]) for me in range(STREAMS)]

    def advance(me):
        try:
            next(lanes[me])
            return True
        except StopIteration:
            return False

    fetches = [("coupling", 0), ("diag", 1), ("coupling", 1), ("coupling", 2), ("diag", 2)]
    step = 0
    alive = True
    while alive:
        alive = False
        for me in range(STREAMS):
            alive = advance(me) or alive
            if fetches and step % 2 == 0:
                bring(*fetches.pop(0))
            for high in range(2, LEVELS):
                for low in range(high - 1):
                    if (low, me) in solved and ("coupling", pair_index(high, low)) in blocks:
                        far_term(high, low, me, solved, LOWER)
                    if (high, me) in answers:
                        far_term(high, low, me, answers, UPPER)
            step += 1
    stack = lambda found: jnp.stack(
        [jnp.concatenate([found[level, me] for me in range(STREAMS)]) for level in range(LEVELS)]
    )
    return stack(answers), stack(solved)


def solution(mesh):
    placed = (
        P("groups", "cols", "rows"),
        P("groups", "rows", "cols"),
        P("groups", None, "cols"),
        P("groups"),
    )
    return jax.shard_map(
        functools.partial(body, sizes=dict(mesh.shape)),
        mesh=mesh,
        in_specs=placed,
        out_specs=(P("groups", None, "cols"), P("groups", None, "rows")),
        check_vma=False,
    )
```

```python
import functools
from typing import NamedTuple

import jax
import jax.numpy as jnp
from jax import lax
from jax.experimental import pallas as pl
from jax.experimental.pallas import tpu as pltpu
from jax.sharding import PartitionSpec as P

LEVELS = 3
COPIES = 8
AHEAD = 2
LANES = 128
DIRECT_MAX = 8
IN_VMEM = pl.BlockSpec(memory_space=pltpu.VMEM)
IN_HBM = pl.BlockSpec(memory_space=pltpu.HBM)
SHORT = pl.CostEstimate(flops=0, transcendentals=0, bytes_accessed=0)
LOWER = (((1,), (1,)), ((), ()))
UPPER = (((1,), (0,)), ((), ()))


def pair_index(high, low):
    return high * (high - 1) // 2 + low


def power_of_two(size):
    return size & (size - 1) == 0


class Piece(NamedTuple):
    axis: str
    away: int
    parts: int

    def span(self, extent):
        width = extent // self.parts
        own = lax.axis_index(self.axis) % self.parts
        return pl.ds(pl.multiple_of((own ^ self.away) * width, LANES), width)


class Job(NamedTuple):
    vectors: list
    places: list
    block: jax.Array
    dims: tuple
    given: list
    outs: list


def in_hbm(blocks):
    return pltpu.with_memory_space_constraint(blocks, pltpu.HBM)


def block_copies(blocks_ref, out_ref, sems, index):
    height = out_ref.shape[0] // COPIES
    return [
        pltpu.make_async_copy(
            blocks_ref.at[index, pl.ds(i * height, height), :],
            out_ref.at[pl.ds(i * height, height), :],
            sems.at[i],
        )
        for i in range(COPIES)
    ]


def work(job, bring):
    operands, in_specs, out_shape, scratch = [], [], [], []
    if job:
        operands += [*job.vectors, *(job.given or ()), job.block]
        in_specs += [IN_VMEM] * len(operands)
        extent = job.block.shape[0 if job.dims is LOWER else 1]
        depth = job.block.shape[1 if job.dims is LOWER else 0]
        rows = job.vectors[0].shape[0]
        out_shape += [
            jax.ShapeDtypeStruct((rows, extent // out.parts), jnp.float32) for out in job.outs
        ]
    if bring:
        operands.append(in_hbm(bring[0]))
        in_specs.append(IN_HBM)
        out_shape.append(jax.ShapeDtypeStruct(bring[0].shape[1:], bring[0].dtype))
        scratch.append(pltpu.SemaphoreType.DMA((COPIES,)))

    def kernel(*refs):
        ins, refs = refs[: len(operands)], refs[len(operands) :]
        outs, refs = refs[: len(out_shape)], refs[len(out_shape) :]
        copies = block_copies(ins[-1], outs[-1], refs[0], bring[1]) if bring else []
        for copy in copies:
            copy.start()
        if job:
            count = len(job.vectors)
            vectors = [ref[...].astype(jnp.bfloat16) for ref in ins[:count]]
            block_ref = ins[count + len(job.given or ())]
            for j, out in enumerate(job.outs):
                total = ins[count + j][...] if job.given else None
                for vector, place in zip(vectors, job.places):
                    inner, outer = place.span(depth), out.span(extent)
                    part = block_ref[outer, inner] if job.dims is LOWER else block_ref[inner, outer]
                    term = lax.dot_general(
                        vector, part, job.dims, preferred_element_type=jnp.float32
                    )
                    total = term if total is None else total + term
                outs[j][...] = total
        for copy in copies:
            copy.wait()

    return pl.pallas_call(
        kernel,
        out_shape=out_shape,
        in_specs=in_specs,
        out_specs=[IN_VMEM] * len(out_shape),
        scratch_shapes=scratch,
        compiler_params=pltpu.CompilerParams(vmem_limit_bytes=2 << 20),
        cost_estimate=SHORT,
        name=("products" if job else "fetch") + ("_fetch" if job and bring else ""),
    )(*operands)


def begin(selector, loads, blocks, out):
    rows, cols = blocks.shape[1:]
    height = rows // out.parts
    copies_of = COPIES // out.parts
    piece = height // copies_of

    def kernel(selector_ref, loads_ref, blocks_ref, out_ref, block_ref, sems):
        start = out.span(rows).start
        copies = [
            pltpu.make_async_copy(
                blocks_ref.at[0, pl.ds(pl.multiple_of(start + i * piece, LANES), piece), :],
                block_ref.at[pl.ds(i * piece, piece), :],
                sems.at[i],
            )
            for i in range(copies_of)
        ]
        for copy in copies[:AHEAD]:
            copy.start()
        vector = jnp.dot(selector_ref[...], loads_ref[0], preferred_element_type=jnp.float32)
        vector_bf = vector.astype(jnp.bfloat16)
        for i, copy in enumerate(copies):
            copy.wait()
            if i + AHEAD < copies_of:
                copies[i + AHEAD].start()
            span = slice(i * piece, (i + 1) * piece)
            out_ref[:, span] = lax.dot_general(
                vector_bf, block_ref[span, :], LOWER, preferred_element_type=jnp.float32
            )

    return pl.pallas_call(
        kernel,
        out_shape=jax.ShapeDtypeStruct((selector.shape[0], height), jnp.float32),
        in_specs=[IN_VMEM, IN_VMEM, IN_HBM],
        out_specs=IN_VMEM,
        scratch_shapes=[
            pltpu.VMEM((height, cols), blocks.dtype),
            pltpu.SemaphoreType.DMA((copies_of,)),
        ],
        compiler_params=pltpu.CompilerParams(vmem_limit_bytes=6 << 20),
        cost_estimate=SHORT,
        name="begin",
    )(selector, loads, in_hbm(blocks))


def select(selector, loads, out):
    def kernel(selector_ref, loads_ref, *out_refs):
        for level, out_ref in enumerate(out_refs, 1):
            out_ref[...] = jnp.dot(
                selector_ref[...],
                loads_ref[level, :, out.span(loads.shape[2])],
                preferred_element_type=jnp.float32,
            )

    shape = jax.ShapeDtypeStruct((selector.shape[0], loads.shape[2] // out.parts), jnp.float32)
    return pl.pallas_call(
        kernel,
        out_shape=[shape] * (LEVELS - 1),
        in_specs=[IN_VMEM, IN_VMEM],
        out_specs=[IN_VMEM] * (LEVELS - 1),
        compiler_params=pltpu.CompilerParams(vmem_limit_bytes=2 << 20),
        cost_estimate=SHORT,
        name="select",
    )(selector, loads)


def place(levels, pieces, places, width, held):
    rows = pieces[0].shape[0]

    def kernel(*refs):
        out_ref, sems = refs[-2:]
        copies = []
        for i, ref in enumerate(refs[: len(pieces)]):
            which, j = divmod(i, len(places))
            target = out_ref.at[levels[which], :, places[j].span(width)]
            copies.append(pltpu.make_async_copy(ref, target, sems.at[i]))
        for copy in copies:
            copy.start()
        for copy in copies:
            copy.wait()

    return pl.pallas_call(
        kernel,
        out_shape=jax.ShapeDtypeStruct((LEVELS, rows, width), jnp.float32),
        in_specs=[IN_VMEM] * len(pieces) + [IN_HBM] * len(held),
        out_specs=IN_HBM,
        scratch_shapes=[pltpu.SemaphoreType.DMA((len(pieces),))],
        input_output_aliases={len(pieces): 0} if held else {},
        compiler_params=pltpu.CompilerParams(vmem_limit_bytes=2 << 20),
        cost_estimate=SHORT,
        name="place",
    )(*pieces, *held)


class Order:
    def __init__(self):
        self.last = ()

    def after(self, *values):
        *values, self.last = lax.optimization_barrier((*values, self.last))
        return values

    def run(self, function, *values):
        self.last = function(*self.after(*values))
        return self.last


def staged(coupling, diag_inverse, loads, selector, n_rows, n_cols):
    order = Order()
    far = list(range(n_rows - 1, n_rows // 2 - 1, -1))
    near = list(range(n_rows // 2 - 1, 0, -1))
    chunk = {k: Piece("rows", k, n_rows) for k in range(n_rows)}
    keep_half, send_half = Piece("cols", 0, 2), Piece("cols", 1, 2)
    blocks = {}

    def products(vectors, places, name, dims, given, outs, bring=None):
        def call(*values):
            job = Job(
                values[: len(vectors)], places, values[len(vectors)], dims, values[len(vectors) + 1 :], outs
            )
            return work(job, source(bring))

        result = list(order.run(call, *vectors, blocks[name], *(given or ())))
        if bring:
            blocks[bring] = result.pop()
        return result

    def source(name):
        return name and (diag_inverse if name[0] == "diag" else coupling, name[1])

    def fetch(name):
        def call():
            if name not in blocks:
                (blocks[name],) = order.run(lambda: work(None, source(name)))

        return call

    def permute(value, axis, step):
        size = n_rows if axis == "rows" else n_cols
        (value,) = order.after(value)
        return lax.ppermute(value, axis, [(i, i ^ step) for i in range(size)])

    def add(*values):
        return order.run(lambda *found: functools.reduce(jnp.add, found), *values)

    def nothing():
        pass

    def cols_sum(keep, got, filler):
        kept = add(keep, got)
        step = 2
        while step < n_cols:
            got = permute(kept, "cols", step)
            filler()
            filler = nothing
            kept = add(kept, got)
            step *= 2
        return kept

    def through_rows(kept, name, dims, given=None, filler=nothing):
        other = permute(kept, "cols", 1)
        ks = far + near + [0]
        parts = products([kept], [keep_half], name, dims, given, [chunk[k] for k in ks])
        parts = dict(zip(ks, parts))

        def finish(ks):
            return products(
                [other], [send_half], name, dims, [parts[k] for k in ks], [chunk[k] for k in ks]
            )

        (other,) = order.after(other)
        got = [permute(part, "rows", k) for k, part in zip(far, finish(far))]
        *rest, own = finish(near + [0])
        got += [permute(part, "rows", k) for k, part in zip(near, rest)]
        filler()
        return other, add(own, *got[::-1])

    def gather(own):
        return {0: own} | {k: permute(own, "rows", k) for k in far + near}

    def through_cols(pieces, name, dims, given=None, bring=None, filler=nothing):
        halves = [send_half, keep_half]
        given = products([pieces[0]], [chunk[0]], name, dims, given, halves, bring)
        for k in near:
            given = products([pieces[k]], [chunk[k]], name, dims, given, halves)
        last = [pieces[k] for k in far], [chunk[k] for k in far]
        (send,) = products(*last, name, dims, given[:1], halves[:1])
        got = permute(send, "cols", 1)
        (keep,) = products(*last, name, dims, given[1:], halves[1:])
        return cols_sum(keep, got, filler)

    assert LEVELS == 3
    pair = lambda high, low: ("coupling", pair_index(high, low))
    send = order.run(lambda a, b: begin(a, b, diag_inverse, send_half), selector, loads)
    got = permute(send, "cols", 1)
    keep = order.run(lambda a, b: begin(a, b, diag_inverse, keep_half), selector, loads)
    rhs_chunks = {}
    skipped = {}

    def skip_forward():
        ks = far + near + [0]
        skipped["forward"] = products(
            solved[0], [keep_half, send_half], pair(2, 0), LOWER, None, [chunk[k] for k in ks], pair(2, 1)
        )

    def skip_backward():
        ks = list(answers[2])
        skipped["backward"] = products(
            [answers[2][k] for k in ks], [chunk[k] for k in ks], pair(2, 0), UPPER, None,
            [send_half, keep_half],
        )

    solved, answers = {}, {}


    def prepare():
        found = order.run(lambda a, b: select(a, b, chunk[0]), selector, loads)
        rhs_chunks.update(enumerate(found, 1))
        fetch(pair(1, 0))()

    kept = cols_sum(keep, got, prepare)
    other, total = through_rows(kept, pair(1, 0), LOWER, None, fetch(("diag", 1)))
    solved[0] = [kept, other]
    pieces = gather(order.run(jnp.subtract, rhs_chunks[1], total))
    kept = through_cols(pieces, ("diag", 1), LOWER, None, pair(2, 0), skip_forward)
    other, total = through_rows(kept, pair(2, 1), LOWER, skipped["forward"], fetch(("diag", 2)))
    solved[1] = [kept, other]
    pieces = gather(order.run(jnp.subtract, rhs_chunks[2], total))
    kept = through_cols(pieces, ("diag", 2), LOWER)
    other, total = through_rows(kept, ("diag", 2), UPPER)
    solved[2] = [kept, other]
    answers[2] = gather(total)
    kept = through_cols(answers[2], pair(2, 1), UPPER, None, None, skip_backward)
    kept = order.run(jnp.subtract, solved[1][0], kept)
    forward = []

    def put_forward():
        pieces = [piece for level in range(LEVELS) for piece in solved[level]]
        width = diag_inverse.shape[1]
        halves = [keep_half, send_half]
        forward.append(
            order.run(lambda *found: place(range(LEVELS), found, halves, width, ()), *pieces)
        )

    def put_influence(levels, held):
        width = diag_inverse.shape[2]
        pieces = [answers[level][k] for level in levels for k in chunk]
        count = len(pieces)
        return order.run(
            lambda *found: place(
                levels, found[:count], list(chunk.values()), width, found[count:]
            ),
            *pieces,
            *held,
        )

    held = []
    _, total = through_rows(kept, ("diag", 1), UPPER, None, fetch(("diag", 0)))
    answers[1] = gather(total)
    kept = through_cols(answers[1], pair(1, 0), UPPER, skipped["backward"], None, put_forward)
    kept = order.run(jnp.subtract, solved[0][0], kept)
    _, total = through_rows(
        kept, ("diag", 0), UPPER, None, lambda: held.append(put_influence([2, 1], ()))
    )
    answers[0] = gather(total)
    influence = put_influence([0], held)
    forward = forward[0]
    return influence, forward


def plain(coupling, diag_inverse, rhs):
    def lower(vector, block):
        return lax.dot_general(
            vector.astype(jnp.bfloat16), block, LOWER, preferred_element_type=jnp.float32
        )

    def upper(vector, block):
        return lax.dot_general(
            vector.astype(jnp.bfloat16), block, UPPER, preferred_element_type=jnp.float32
        )

    solved, answers = {}, {}
    for level in range(LEVELS):
        resid = rhs[level]
        if level:
            terms = [lower(solved[j], coupling[pair_index(level, j)]) for j in range(level)]
            resid = resid - lax.psum(functools.reduce(jnp.add, terms), "rows")
        solved[level] = lax.psum(lower(resid, diag_inverse[level]), "cols")
    for level in range(LEVELS - 1, -1, -1):
        resid = solved[level]
        if level < LEVELS - 1:
            terms = [
                upper(answers[j], coupling[pair_index(j, level)]) for j in range(level + 1, LEVELS)
            ]
            resid = resid - lax.psum(functools.reduce(jnp.add, terms), "cols")
        answers[level] = lax.psum(upper(resid, diag_inverse[level]), "rows")
    stack = lambda found: jnp.stack([found[level] for level in range(LEVELS)])
    return stack(answers), stack(solved)


def body(coupling, diag_inverse, loads, axle_index, *, n_rows, n_cols):
    positions = loads.shape[1]
    selector = (axle_index[:, None] == jnp.arange(positions, dtype=jnp.int32)[None, :]).astype(
        jnp.bfloat16
    )
    over_rows, over_cols = diag_inverse.shape[1:]
    if (
        power_of_two(n_rows)
        and power_of_two(n_cols)
        and 1 < n_rows <= DIRECT_MAX
        and n_cols > 1
        and over_cols % (n_rows * LANES) == 0
        and over_rows % (COPIES * LANES) == 0
    ):
        return staged(coupling, diag_inverse, loads, selector, n_rows, n_cols)
    rhs = jnp.einsum("lp,kpc->klc", selector, loads, preferred_element_type=jnp.float32)
    return plain(coupling, diag_inverse, rhs)


def solution(mesh):
    placed = (
        P("groups", "cols", "rows"),
        P("groups", "rows", "cols"),
        P("groups", None, "cols"),
        P("groups"),
    )
    return jax.shard_map(
        functools.partial(body, n_rows=mesh.shape["rows"], n_cols=mesh.shape["cols"]),
        mesh=mesh,
        in_specs=placed,
        out_specs=(P("groups", None, "cols"), P("groups", None, "rows")),
        check_vma=False,
    )
```

```python
import functools
from typing import NamedTuple

import jax
import jax.numpy as jnp
from jax import lax
from jax.experimental import pallas as pl
from jax.experimental.pallas import tpu as pltpu
from jax.sharding import PartitionSpec as P

LEVELS = 3
COPIES = 8
LANES = 128
CHUNKS = 2
IN_VMEM = pl.BlockSpec(memory_space=pltpu.VMEM)
IN_HBM = pl.BlockSpec(memory_space=pltpu.HBM)
SHORT = pl.CostEstimate(flops=0, transcendentals=0, bytes_accessed=0)
LOWER = (((1,), (1,)), ((), ()))
UPPER = (((1,), (0,)), ((), ()))


def pair_index(high, low):
    return high * (high - 1) // 2 + low


def power_of_two(size):
    return size & (size - 1) == 0


class Part(NamedTuple):
    axis: str
    away: int
    chunk: int = 0
    chunks: int = 1

    def span(self, extent):
        width = extent // 2
        at = lax.axis_index(self.axis)
        if self.axis == "rows":
            at = at ^ (at >> 1)
        inner = width // self.chunks
        start = ((at & 1) ^ self.away) * width + self.chunk * inner
        return pl.ds(pl.multiple_of(start, LANES), inner)

    def width(self, extent):
        return extent // (2 * self.chunks)


class Whole(NamedTuple):
    def span(self, extent):
        return pl.ds(0, extent)


class Job(NamedTuple):
    vectors: list
    places: list
    block: jax.Array
    dims: tuple
    given: list
    outs: list


def in_hbm(blocks):
    return pltpu.with_memory_space_constraint(blocks, pltpu.HBM)


def block_copies(blocks_ref, out_ref, sems, index):
    height = out_ref.shape[0] // COPIES
    return [
        pltpu.make_async_copy(
            blocks_ref.at[index, pl.ds(i * height, height), :],
            out_ref.at[pl.ds(i * height, height), :],
            sems.at[i],
        )
        for i in range(COPIES)
    ]


def work(job, bring):
    operands, in_specs, out_shape, scratch = [], [], [], []
    if job:
        operands += [*job.vectors, *(job.given or ()), job.block]
        in_specs += [IN_VMEM] * len(operands)
        extent = job.block.shape[0 if job.dims is LOWER else 1]
        depth = job.block.shape[1 if job.dims is LOWER else 0]
        rows = job.vectors[0].shape[0]
        out_shape += [
            jax.ShapeDtypeStruct((rows, out.width(extent)), jnp.float32) for out in job.outs
        ]
    if bring:
        operands.append(in_hbm(bring[0]))
        in_specs.append(IN_HBM)
        out_shape.append(jax.ShapeDtypeStruct(bring[0].shape[1:], bring[0].dtype))
        scratch.append(pltpu.SemaphoreType.DMA((COPIES,)))

    def kernel(*refs):
        ins, refs = refs[: len(operands)], refs[len(operands) :]
        outs, refs = refs[: len(out_shape)], refs[len(out_shape) :]
        copies = block_copies(ins[-1], outs[-1], refs[0], bring[1]) if bring else []
        for copy in copies:
            copy.start()
        if job:
            count = len(job.vectors)
            vectors = [ref[...].astype(jnp.bfloat16) for ref in ins[:count]]
            block_ref = ins[count + len(job.given or ())]
            for j, out in enumerate(job.outs):
                total = ins[count + j][...] if job.given else None
                for vector, place in zip(vectors, job.places):
                    inner, outer = place.span(depth), out.span(extent)
                    part = block_ref[outer, inner] if job.dims is LOWER else block_ref[inner, outer]
                    term = lax.dot_general(
                        vector, part, job.dims, preferred_element_type=jnp.float32
                    )
                    total = term if total is None else total + term
                outs[j][...] = total
        for copy in copies:
            copy.wait()

    return pl.pallas_call(
        kernel,
        out_shape=out_shape,
        in_specs=in_specs,
        out_specs=[IN_VMEM] * len(out_shape),
        scratch_shapes=scratch,
        compiler_params=pltpu.CompilerParams(vmem_limit_bytes=2 << 20),
        cost_estimate=SHORT,
        name=("products" if job else "fetch") + ("_fetch" if job and bring else ""),
    )(*operands)


def begin(axle_index, loads, blocks, out):
    rows, cols = blocks.shape[1:]
    height = rows // 2
    count, positions = axle_index.shape[0], loads.shape[1]
    piece = rows // COPIES
    first = height // piece

    def kernel(index_ref, loads_ref, blocks_ref, *refs):
        selector_ref, vector_ref, part_ref, block_ref, index, table, small_sems, sems = refs
        start = out.span(rows).start
        spans = [
            pl.ds(pl.multiple_of((start + i * piece) % rows, piece), piece) for i in range(COPIES)
        ]
        copies = [
            pltpu.make_async_copy(blocks_ref.at[0, span, :], block_ref.at[span, :], sems.at[i])
            for i, span in enumerate(spans)
        ]
        small = [
            pltpu.make_async_copy(index_ref, index, small_sems.at[0]),
            pltpu.make_async_copy(loads_ref.at[0], table, small_sems.at[1]),
        ]
        for copy in small + copies[:first]:
            copy.start()
        for copy in small:
            copy.wait()
        line = lax.broadcasted_iota(jnp.int32, (count, positions), 0)
        wanted = jnp.zeros((count, positions), jnp.int32)
        for i in range(count):
            wanted = jnp.where(line == i, index[i], wanted)
        here = lax.broadcasted_iota(jnp.int32, (count, positions), 1)
        selector = jnp.where(wanted == here, 1.0, 0.0)
        selector_ref[...] = selector
        vector = jnp.dot(
            selector.astype(loads.dtype), table[...], preferred_element_type=jnp.float32
        )
        vector_ref[...] = vector
        for copy in copies[:first]:
            copy.wait()
        for copy in copies[first:]:
            copy.start()
        part_ref[...] = lax.dot_general(
            vector.astype(blocks.dtype),
            block_ref[pl.ds(pl.multiple_of(start, LANES), height), :],
            LOWER,
            preferred_element_type=jnp.float32,
        )
        for copy in copies[first:]:
            copy.wait()

    return pl.pallas_call(
        kernel,
        out_shape=(
            jax.ShapeDtypeStruct((count, positions), jnp.float32),
            jax.ShapeDtypeStruct((count, cols), jnp.float32),
            jax.ShapeDtypeStruct((count, height), jnp.float32),
            jax.ShapeDtypeStruct((rows, cols), blocks.dtype),
        ),
        in_specs=[IN_HBM] * 3,
        out_specs=[IN_VMEM] * 4,
        scratch_shapes=[
            pltpu.SMEM((count,), jnp.int32),
            pltpu.VMEM((positions, cols), loads.dtype),
            pltpu.SemaphoreType.DMA((2,)),
            pltpu.SemaphoreType.DMA((COPIES,)),
        ],
        compiler_params=pltpu.CompilerParams(vmem_limit_bytes=3 << 20),
        cost_estimate=SHORT,
        name="begin",
    )(in_hbm(axle_index), in_hbm(loads), in_hbm(blocks))


def select(selector, loads, outs):
    found = [(level, out) for level, parts in outs.items() for out in parts]

    def kernel(selector_ref, loads_ref, *out_refs):
        for (level, out), out_ref in zip(found, out_refs):
            out_ref[...] = jnp.dot(
                selector_ref[...].astype(loads.dtype),
                loads_ref[level, :, out.span(loads.shape[2])],
                preferred_element_type=jnp.float32,
            )

    result = pl.pallas_call(
        kernel,
        out_shape=[
            jax.ShapeDtypeStruct((selector.shape[0], out.width(loads.shape[2])), jnp.float32)
            for _, out in found
        ],
        in_specs=[IN_VMEM, IN_VMEM],
        out_specs=[IN_VMEM] * len(found),
        compiler_params=pltpu.CompilerParams(vmem_limit_bytes=2 << 20),
        cost_estimate=SHORT,
        name="select",
    )(selector, loads)
    return {key: [r for (level, _), r in zip(found, result) if level == key] for key in outs}


def place(pieces, targets, width, held):
    rows = pieces[0].shape[0]

    def kernel(*refs):
        out_ref, sems = refs[-2:]
        copies = [
            pltpu.make_async_copy(ref, out_ref.at[level, :, part.span(width)], sems.at[i])
            for i, (ref, (level, part)) in enumerate(zip(refs, targets))
        ]
        for copy in copies:
            copy.start()
        for copy in copies:
            copy.wait()

    return pl.pallas_call(
        kernel,
        out_shape=jax.ShapeDtypeStruct((LEVELS, rows, width), jnp.float32),
        in_specs=[IN_VMEM] * len(pieces) + [IN_HBM] * len(held),
        out_specs=IN_HBM,
        scratch_shapes=[pltpu.SemaphoreType.DMA((len(pieces),))],
        input_output_aliases={len(pieces): 0} if held else {},
        compiler_params=pltpu.CompilerParams(vmem_limit_bytes=2 << 20),
        cost_estimate=SHORT,
        name="place",
    )(*pieces, *held)


class Order:
    def __init__(self):
        self.last = ()

    def after(self, *values):
        *values, self.last = lax.optimization_barrier((*values, self.last))
        return values

    def run(self, function, *values):
        self.last = function(*self.after(*values))
        return self.last


def staged(coupling, diag_inverse, loads, axle_index, sizes):
    order = Order()
    blocks = {}
    steps = {axis: [1 << i for i in range(1, size.bit_length() - 1)] for axis, size in sizes.items()}
    steps["rows"] = [3 if step == 2 else step for step in steps["rows"]]

    def parts(axis, away, chunks):
        return [Part(axis, away, chunk, chunks) for chunk in range(chunks)]

    def source(name):
        return name and (diag_inverse if name[0] == "diag" else coupling, name[1])

    def products(vectors, places, name, dims, given, outs):
        count = len(vectors)

        def call(*values):
            job = Job(values[:count], places, values[count], dims, values[count + 1 :], outs)
            return work(job, None)

        return list(order.run(call, *vectors, blocks[name], *(given or ())))

    def fetch(name):
        def call():
            (blocks[name],) = order.run(lambda: work(None, source(name)))

        return call

    def permute(value, axis, step):
        (value,) = order.after(value)
        return lax.ppermute(value, axis, [(i, i ^ step) for i in range(sizes[axis])])

    def nothing():
        pass

    def phase(axis, chunks, finish, onward, early=nothing, middle=nothing, late=nothing, post=None):
        every = range(chunks)
        got = [permute(finish([i])[0], axis, 1) for i in every]
        kept = finish([chunks + i for i in every])
        early()
        for step in [*steps[axis], None]:
            sent = []
            for i in every:
                kept[i] = order.run(jnp.add, kept[i], got[i])
                if step is None and post is not None:
                    kept[i] = order.run(jnp.subtract, post()[i], kept[i])
                sent.append(permute(kept[i], axis, step or 1))
            got = sent
            if step is not None:
                middle()
                middle = nothing
        own, others = parts(axis, 0, chunks), parts(axis, 1, chunks)
        if onward is None:
            late(kept)
            return kept, got, None
        name, dims, next_chunks, given = onward
        away = "cols" if axis == "rows" else "rows"
        outs = parts(away, 1, next_chunks) + parts(away, 0, next_chunks)
        given = products(kept, own, name, dims, given and given(), outs)
        late()
        for i in every[:-1]:
            (got[i],) = order.after(got[i])
            given = products(got[i : i + 1], others[i : i + 1], name, dims, given, outs)
        (got[-1],) = order.after(got[-1])

        def rest(which):
            return products(
                got[-1:], others[-1:], name, dims, [given[i] for i in which], [outs[i] for i in which]
            )

        return kept, got, rest

    def pair(high, low):
        return "coupling", pair_index(high, low)

    chunks = {level: 1 if level == 1 else CHUNKS for level in range(1, LEVELS)}
    selector, vector, first, blocks["diag", 0] = order.run(
        lambda: begin(axle_index, loads, diag_inverse, Part("cols", 1))
    )
    rhs, solved, answers, skipped, done = {}, {}, {}, {}, {}

    def first_finish(which):
        if which == [0]:
            return [first]
        return products([vector], [Whole()], ("diag", 0), LOWER, None, [Part("cols", 0)])

    def prepare():
        del blocks["diag", 0]
        wanted = {level: parts("rows", 0, count) for level, count in chunks.items()}
        rhs.update(order.run(lambda a, b: select(a, b, wanted), selector, loads))
        fetch(pair(1, 0))()

    def skip_forward():
        outs = parts("rows", 1, CHUNKS) + parts("rows", 0, CHUNKS)
        skipped[LOWER] = products(
            sum(solved[0], []), parts("cols", 0, 1) + parts("cols", 1, 1), pair(2, 0), LOWER, None, outs
        )

    def skip_backward():
        outs = parts("cols", 1, 1) + parts("cols", 0, 1)
        places = parts("rows", 0, CHUNKS) + parts("rows", 1, CHUNKS)
        skipped[UPPER] = products(sum(answers[2], []), places, pair(2, 0), UPPER, None, outs)

    def put(found, levels, axis, count, halves=(0, 1), held=()):
        width = diag_inverse.shape[2 if axis == "rows" else 1]
        pieces = [piece for level in levels for half in halves for piece in found[level][half]]
        targets = [
            (level, part) for level in levels for half in halves for part in parts(axis, half, count)
        ]
        number = len(pieces)
        return order.run(
            lambda *values: place(values[:number], targets, width, values[number:]), *pieces, *held
        )

    def put_forward():
        done["forward"] = put(solved, range(LEVELS), "cols", 1)

    def put_early():
        done["early"] = put(answers, [2, 1], "rows", CHUNKS)

    def put_own(kept):
        done["own"] = put({0: [kept]}, [0], "rows", CHUNKS, [0], [done["early"]])

    *solved[0], finish = phase(
        "cols", 1, first_finish, (pair(1, 0), LOWER, chunks[1], None), middle=prepare
    )
    *_, finish = phase(
        "rows", chunks[1], finish, (("diag", 1), LOWER, 1, None),
        fetch(("diag", 1)), fetch(pair(2, 0)), skip_forward, lambda: rhs[1],
    )
    *solved[1], finish = phase(
        "cols", 1, finish, (pair(2, 1), LOWER, chunks[2], lambda: skipped[LOWER]),
        middle=fetch(pair(2, 1)),
    )
    *_, finish = phase(
        "rows", chunks[2], finish, (("diag", 2), LOWER, 1, None),
        middle=fetch(("diag", 2)), post=lambda: rhs[2],
    )
    *solved[2], finish = phase("cols", 1, finish, (("diag", 2), UPPER, CHUNKS, None))
    *answers[2], finish = phase("rows", CHUNKS, finish, (pair(2, 1), UPPER, 1, None))
    *_, finish = phase(
        "cols", 1, finish, (("diag", 1), UPPER, CHUNKS, None),
        middle=skip_backward, post=lambda: solved[1][0],
    )
    *answers[1], finish = phase(
        "rows", CHUNKS, finish, (pair(1, 0), UPPER, 1, lambda: skipped[UPPER]),
        middle=fetch(("diag", 0)),
    )
    *_, finish = phase(
        "cols", 1, finish, (("diag", 0), UPPER, CHUNKS, None),
        middle=put_forward, post=lambda: solved[0][0],
    )
    *answers[0], _ = phase("rows", CHUNKS, finish, None, middle=put_early, late=put_own)
    influence = put(answers, [0], "rows", CHUNKS, [1], [done["own"]])
    return influence, done["forward"]


def plain(coupling, diag_inverse, rhs):
    def lower(vector, block):
        return lax.dot_general(
            vector.astype(jnp.bfloat16), block, LOWER, preferred_element_type=jnp.float32
        )

    def upper(vector, block):
        return lax.dot_general(
            vector.astype(jnp.bfloat16), block, UPPER, preferred_element_type=jnp.float32
        )

    solved, answers = {}, {}
    for level in range(LEVELS):
        resid = rhs[level]
        if level:
            terms = [lower(solved[j], coupling[pair_index(level, j)]) for j in range(level)]
            resid = resid - lax.psum(functools.reduce(jnp.add, terms), "rows")
        solved[level] = lax.psum(lower(resid, diag_inverse[level]), "cols")
    for level in range(LEVELS - 1, -1, -1):
        resid = solved[level]
        if level < LEVELS - 1:
            terms = [
                upper(answers[j], coupling[pair_index(j, level)]) for j in range(level + 1, LEVELS)
            ]
            resid = resid - lax.psum(functools.reduce(jnp.add, terms), "cols")
        answers[level] = lax.psum(upper(resid, diag_inverse[level]), "rows")
    stack = lambda found: jnp.stack([found[level] for level in range(LEVELS)])
    return stack(answers), stack(solved)


def body(coupling, diag_inverse, loads, axle_index, *, n_rows, n_cols):
    over_rows, over_cols = diag_inverse.shape[1:]
    if (
        power_of_two(n_rows)
        and power_of_two(n_cols)
        and min(n_rows, n_cols) > 1
        and over_cols % (2 * CHUNKS * LANES) == 0
        and over_rows % (2 * LANES) == 0
    ):
        sizes = {"rows": n_rows, "cols": n_cols}
        return staged(coupling, diag_inverse, loads, axle_index, sizes)
    positions = loads.shape[1]
    selector = (axle_index[:, None] == jnp.arange(positions, dtype=jnp.int32)[None, :]).astype(
        jnp.bfloat16
    )
    rhs = jnp.einsum("lp,kpc->klc", selector, loads, preferred_element_type=jnp.float32)
    return plain(coupling, diag_inverse, rhs)


def solution(mesh):
    placed = (
        P("groups", "cols", "rows"),
        P("groups", "rows", "cols"),
        P("groups", None, "cols"),
        P("groups"),
    )
    return jax.shard_map(
        functools.partial(body, n_rows=mesh.shape["rows"], n_cols=mesh.shape["cols"]),
        mesh=mesh,
        in_specs=placed,
        out_specs=(P("groups", None, "cols"), P("groups", None, "rows")),
        check_vma=False,
    )
```

```python
import functools
from typing import NamedTuple

import jax
import jax.numpy as jnp
from jax import lax
from jax.experimental import pallas as pl
from jax.experimental.pallas import tpu as pltpu
from jax.sharding import PartitionSpec as P

LEVELS = 3
COPIES = 8
LANES = 128
CHUNKS = 2
IN_VMEM = pl.BlockSpec(memory_space=pltpu.VMEM)
IN_HBM = pl.BlockSpec(memory_space=pltpu.HBM)
SHORT = pl.CostEstimate(flops=0, transcendentals=0, bytes_accessed=0)
LOWER = (((1,), (1,)), ((), ()))
UPPER = (((1,), (0,)), ((), ()))


def pair_index(high, low):
    return high * (high - 1) // 2 + low


def power_of_two(size):
    return size & (size - 1) == 0


class Part(NamedTuple):
    axis: str
    away: int
    chunk: int = 0
    chunks: int = 1

    def span(self, extent):
        width = extent // 2
        at = lax.axis_index(self.axis)
        if self.axis == "rows":
            at = at >> (lax.axis_index("cols") & 1)
        inner = width // self.chunks
        start = ((at & 1) ^ self.away) * width + self.chunk * inner
        return pl.ds(pl.multiple_of(start, LANES), inner)

    def width(self, extent):
        return extent // (2 * self.chunks)


class Whole(NamedTuple):
    def span(self, extent):
        return pl.ds(0, extent)


class Job(NamedTuple):
    vectors: list
    places: list
    block: jax.Array
    dims: tuple
    given: list
    outs: list


def in_hbm(blocks):
    return pltpu.with_memory_space_constraint(blocks, pltpu.HBM)


def block_copies(blocks_ref, out_ref, sems, index, pieces):
    height = out_ref.shape[0] // COPIES
    return [
        pltpu.make_async_copy(
            blocks_ref.at[index, pl.ds(i * height, height), :],
            out_ref.at[pl.ds(i * height, height), :],
            sems.at[i],
        )
        for i in pieces
    ]


class Bring(NamedTuple):
    blocks: jax.Array
    index: int
    pieces: range
    held: list


def work(job, bring):
    operands, in_specs, out_shape, scratch, aliases = [], [], [], [], {}
    if job:
        known = [j for j, value in enumerate(job.given) if value is not None]
        operands += [*job.vectors, *(job.given[j] for j in known), job.block]
        in_specs += [IN_VMEM] * len(operands)
        extent = job.block.shape[0 if job.dims is LOWER else 1]
        depth = job.block.shape[1 if job.dims is LOWER else 0]
        rows = job.vectors[0].shape[0]
        out_shape += [
            jax.ShapeDtypeStruct((rows, out.width(extent)), jnp.float32) for out in job.outs
        ]
    if bring:
        aliases = {len(operands): len(out_shape)} if bring.held else {}
        operands += [*bring.held, in_hbm(bring.blocks)]
        in_specs += [IN_VMEM] * len(bring.held) + [IN_HBM]
        out_shape.append(jax.ShapeDtypeStruct(bring.blocks.shape[1:], bring.blocks.dtype))
        scratch.append(pltpu.SemaphoreType.DMA((COPIES,)))

    def kernel(*refs):
        ins, refs = refs[: len(operands)], refs[len(operands) :]
        outs, refs = refs[: len(out_shape)], refs[len(out_shape) :]
        copies = []
        if bring:
            copies = block_copies(ins[-1], outs[-1], refs[0], bring.index, bring.pieces)
        for copy in copies:
            copy.start()
        if job:
            count = len(job.vectors)
            vectors = [ref[...].astype(jnp.bfloat16) for ref in ins[:count]]
            given = dict(zip(known, ins[count:]))
            block_ref = ins[count + len(known)]
            for j, out in enumerate(job.outs):
                total = given[j][...] if j in given else None
                for vector, place in zip(vectors, job.places):
                    inner, outer = place.span(depth), out.span(extent)
                    part = block_ref[outer, inner] if job.dims is LOWER else block_ref[inner, outer]
                    term = lax.dot_general(
                        vector, part, job.dims, preferred_element_type=jnp.float32
                    )
                    total = term if total is None else total + term
                outs[j][...] = total
        for copy in copies:
            copy.wait()

    return pl.pallas_call(
        kernel,
        out_shape=out_shape,
        in_specs=in_specs,
        out_specs=[IN_VMEM] * len(out_shape),
        scratch_shapes=scratch,
        input_output_aliases=aliases,
        compiler_params=pltpu.CompilerParams(vmem_limit_bytes=2 << 20),
        cost_estimate=SHORT,
        name=("products" if job else "fetch") + ("_fetch" if job and bring else ""),
    )(*operands)


def begin(axle_index, loads, blocks, out):
    rows, cols = blocks.shape[1:]
    height = rows // 2
    count, positions = axle_index.shape[0], loads.shape[1]
    piece = rows // COPIES
    first = height // piece

    def kernel(index_ref, loads_ref, blocks_ref, *refs):
        selector_ref, vector_ref, part_ref, block_ref, index, table, small_sems, sems = refs
        start = out.span(rows).start
        spans = [
            pl.ds(pl.multiple_of((start + i * piece) % rows, piece), piece) for i in range(COPIES)
        ]
        copies = [
            pltpu.make_async_copy(blocks_ref.at[0, span, :], block_ref.at[span, :], sems.at[i])
            for i, span in enumerate(spans)
        ]
        small = [
            pltpu.make_async_copy(index_ref, index, small_sems.at[0]),
            pltpu.make_async_copy(loads_ref.at[0], table, small_sems.at[1]),
        ]
        for copy in small + copies:
            copy.start()
        for copy in small:
            copy.wait()
        line = lax.broadcasted_iota(jnp.int32, (count, positions), 0)
        wanted = jnp.zeros((count, positions), jnp.int32)
        for i in range(count):
            wanted = jnp.where(line == i, index[i], wanted)
        here = lax.broadcasted_iota(jnp.int32, (count, positions), 1)
        selector = jnp.where(wanted == here, 1.0, 0.0)
        selector_ref[...] = selector
        vector = jnp.dot(
            selector.astype(loads.dtype), table[...], preferred_element_type=jnp.float32
        )
        vector_ref[...] = vector
        for copy in copies[:first]:
            copy.wait()
        part_ref[...] = lax.dot_general(
            vector.astype(blocks.dtype),
            block_ref[pl.ds(pl.multiple_of(start, LANES), height), :],
            LOWER,
            preferred_element_type=jnp.float32,
        )
        for copy in copies[first:]:
            copy.wait()

    return pl.pallas_call(
        kernel,
        out_shape=(
            jax.ShapeDtypeStruct((count, positions), jnp.float32),
            jax.ShapeDtypeStruct((count, cols), jnp.float32),
            jax.ShapeDtypeStruct((count, height), jnp.float32),
            jax.ShapeDtypeStruct((rows, cols), blocks.dtype),
        ),
        in_specs=[IN_HBM] * 3,
        out_specs=[IN_VMEM] * 4,
        scratch_shapes=[
            pltpu.SMEM((count,), jnp.int32),
            pltpu.VMEM((positions, cols), loads.dtype),
            pltpu.SemaphoreType.DMA((2,)),
            pltpu.SemaphoreType.DMA((COPIES,)),
        ],
        compiler_params=pltpu.CompilerParams(vmem_limit_bytes=3 << 20),
        cost_estimate=SHORT,
        name="begin",
    )(in_hbm(axle_index), in_hbm(loads), in_hbm(blocks))


def select(selector, loads, outs):
    found = [(level, out) for level, parts in outs.items() for out in parts]

    def kernel(selector_ref, loads_ref, *out_refs):
        for (level, out), out_ref in zip(found, out_refs):
            out_ref[...] = jnp.dot(
                selector_ref[...].astype(loads.dtype),
                loads_ref[level, :, out.span(loads.shape[2])],
                preferred_element_type=jnp.float32,
            )

    result = pl.pallas_call(
        kernel,
        out_shape=[
            jax.ShapeDtypeStruct((selector.shape[0], out.width(loads.shape[2])), jnp.float32)
            for _, out in found
        ],
        in_specs=[IN_VMEM, IN_VMEM],
        out_specs=[IN_VMEM] * len(found),
        compiler_params=pltpu.CompilerParams(vmem_limit_bytes=2 << 20),
        cost_estimate=SHORT,
        name="select",
    )(selector, loads)
    return {key: [r for (level, _), r in zip(found, result) if level == key] for key in outs}


def place(pieces, targets, width, held):
    rows = pieces[0].shape[0]

    def kernel(*refs):
        out_ref, sems = refs[-2:]
        copies = [
            pltpu.make_async_copy(ref, out_ref.at[level, :, part.span(width)], sems.at[i])
            for i, (ref, (level, part)) in enumerate(zip(refs, targets))
        ]
        for copy in copies:
            copy.start()
        for copy in copies:
            copy.wait()

    return pl.pallas_call(
        kernel,
        out_shape=jax.ShapeDtypeStruct((LEVELS, rows, width), jnp.float32),
        in_specs=[IN_VMEM] * len(pieces) + [IN_HBM] * len(held),
        out_specs=IN_HBM,
        scratch_shapes=[pltpu.SemaphoreType.DMA((len(pieces),))],
        input_output_aliases={len(pieces): 0} if held else {},
        compiler_params=pltpu.CompilerParams(vmem_limit_bytes=2 << 20),
        cost_estimate=SHORT,
        name="place",
    )(*pieces, *held)


class Order:
    def __init__(self):
        self.last = ()

    def after(self, *values):
        *values, self.last = lax.optimization_barrier((*values, self.last))
        return values

    def run(self, function, *values):
        self.last = function(*self.after(*values))
        return self.last


def staged(coupling, diag_inverse, loads, axle_index, sizes):
    order = Order()
    blocks = {}
    def steps(axis, col=0):
        found = [1 << i for i in range(sizes[axis].bit_length() - 1)]
        if axis == "rows" and col % 2:
            found[:2] = [3, 1]
        return found

    def parts(axis, away, chunks):
        return [Part(axis, away, chunk, chunks) for chunk in range(chunks)]

    def taking(bring):
        if not bring:
            return []
        return [blocks[bring[0]]] if bring[0] in blocks else []

    def source(bring, held):
        if not bring:
            return None
        (kind, index), pieces = bring
        return Bring(diag_inverse if kind == "diag" else coupling, index, pieces, held)

    def products(vectors, places, name, dims, given, outs, bring=None):
        count = len(vectors)
        known = [value for value in given or () if value is not None]
        held = taking(bring)

        def call(*values):
            left = iter(values[count + 1 :])
            terms = [None if value is None else next(left) for value in given or ()]
            job = Job(values[:count], places, values[count], dims, terms, outs)
            return work(job, source(bring, list(left)))

        result = list(order.run(call, *vectors, blocks[name], *known, *held))
        if bring:
            blocks[bring[0]] = result.pop()
        return result

    def fetch(name, pieces=range(COPIES)):
        def call():
            bring = name, pieces
            held = taking(bring)
            (blocks[name],) = order.run(lambda *found: work(None, source(bring, list(found))), *held)

        return call

    def permute(value, axis, number):
        (value,) = order.after(value)
        if axis == "cols":
            step = steps(axis)[number]
            return lax.ppermute(value, axis, [(i, i ^ step) for i in range(sizes[axis])])
        n_cols = sizes["cols"]
        moves = [
            (row * n_cols + col, (row ^ steps(axis, col)[number]) * n_cols + col)
            for row in range(sizes[axis])
            for col in range(n_cols)
        ]
        return lax.ppermute(value, ("rows", "cols"), moves)

    def nothing():
        pass

    def phase(
        axis, chunks, finish, onward, early=nothing, middle=nothing, late=nothing, post=None, during=None
    ):
        every = range(chunks)
        got = [permute(finish([i])[0], axis, 0) for i in every]
        kept = finish([chunks + i for i in every], during)
        more = early()
        if more:
            kept = [order.run(jnp.add, value, term) for value, term in zip(kept, more)]
        last = len(steps(axis))
        for number in range(1, last + 1):
            sent = []
            for i in every:
                kept[i] = order.run(jnp.add, kept[i], got[i])
                if number == last and post is not None:
                    kept[i] = order.run(jnp.subtract, post()[i], kept[i])
                sent.append(permute(kept[i], axis, number % last))
            got = sent
            if number < last:
                middle()
                middle = nothing
        own, others = parts(axis, 0, chunks), parts(axis, 1, chunks)
        if onward is None:
            late(kept)
            return kept, got, None
        name, dims, next_chunks, given = onward
        away = "cols" if axis == "rows" else "rows"
        outs = parts(away, 1, next_chunks) + parts(away, 0, next_chunks)
        extra = given and given()
        given = products(kept, own, name, dims, extra and extra + [None] * (len(outs) - len(extra)), outs)
        late()
        for i in every[:-1]:
            (got[i],) = order.after(got[i])
            given = products(got[i : i + 1], others[i : i + 1], name, dims, given, outs)
        (got[-1],) = order.after(got[-1])

        def rest(which, bring=None):
            terms = [given[i] for i in which]
            return products(
                got[-1:], others[-1:], name, dims, terms, [outs[i] for i in which], bring
            )

        return kept, got, rest

    def pair(high, low):
        return "coupling", pair_index(high, low)

    chunks = {level: 1 if level == 1 else CHUNKS for level in range(1, LEVELS)}
    selector, vector, first, blocks["diag", 0] = order.run(
        lambda: begin(axle_index, loads, diag_inverse, Part("cols", 1))
    )
    rhs, solved, answers, skipped, done = {}, {}, {}, {}, {}

    def first_finish(which, bring=None):
        if which == [0]:
            return [first]
        return products([vector], [Whole()], ("diag", 0), LOWER, None, [Part("cols", 0)])

    def prepare():
        del blocks["diag", 0]
        wanted = {level: parts("rows", 0, count) for level, count in chunks.items()}
        rhs.update(order.run(lambda a, b: select(a, b, wanted), selector, loads))
        fetch(pair(1, 0))()

    def skip_forward(away, bring=None):
        def call():
            places = parts("cols", 0, 1) + parts("cols", 1, 1)
            skipped[LOWER, away] = products(
                sum(solved[0], []), places, pair(2, 0), LOWER, None, parts("rows", away, chunks[2]), bring
            )
            return skipped[LOWER, away]

        return call

    def skip_backward():
        outs = parts("cols", 1, 1) + parts("cols", 0, 1)
        places = parts("rows", 0, CHUNKS) + parts("rows", 1, CHUNKS)
        skipped[UPPER] = products(sum(answers[2], []), places, pair(2, 0), UPPER, None, outs)

    def put(found, levels, axis, count, halves=(0, 1), held=()):
        width = diag_inverse.shape[2 if axis == "rows" else 1]
        pieces = [piece for level in levels for half in halves for piece in found[level][half]]
        targets = [
            (level, part) for level in levels for half in halves for part in parts(axis, half, count)
        ]
        number = len(pieces)
        return order.run(
            lambda *values: place(values[:number], targets, width, values[number:]), *pieces, *held
        )

    def put_forward():
        done["forward"] = put(solved, range(LEVELS), "cols", 1)

    def put_early():
        done["early"] = put(answers, [2, 1], "rows", CHUNKS)

    def put_own(kept):
        done["own"] = put({0: [kept]}, [0], "rows", CHUNKS, [0], [done["early"]])

    *solved[0], finish = phase(
        "cols", 1, first_finish, (pair(1, 0), LOWER, chunks[1], None), middle=prepare
    )
    *_, finish = phase(
        "rows", chunks[1], finish, (("diag", 1), LOWER, 1, None),
        middle=fetch(pair(2, 0)), late=skip_forward(1), post=lambda: rhs[1],
        during=(("diag", 1), range(COPIES)),
    )
    *solved[1], finish = phase(
        "cols", 1, finish, (pair(2, 1), LOWER, chunks[2], lambda: skipped[LOWER, 1]),
        middle=fetch(pair(2, 1)),
    )
    *_, finish = phase(
        "rows", chunks[2], finish, (("diag", 2), LOWER, 1, None),
        early=skip_forward(0), middle=fetch(("diag", 2)), post=lambda: rhs[2],
    )
    *solved[2], finish = phase("cols", 1, finish, (("diag", 2), UPPER, CHUNKS, None))
    *answers[2], finish = phase("rows", CHUNKS, finish, (pair(2, 1), UPPER, 1, None))
    *_, finish = phase(
        "cols", 1, finish, (("diag", 1), UPPER, CHUNKS, None),
        middle=skip_backward, post=lambda: solved[1][0],
    )
    *answers[1], finish = phase(
        "rows", CHUNKS, finish, (pair(1, 0), UPPER, 1, lambda: skipped[UPPER]),
        middle=fetch(("diag", 0)),
    )
    *_, finish = phase(
        "cols", 1, finish, (("diag", 0), UPPER, CHUNKS, None),
        middle=put_forward, post=lambda: solved[0][0],
    )
    *answers[0], _ = phase("rows", CHUNKS, finish, None, middle=put_early, late=put_own)
    influence = put(answers, [0], "rows", CHUNKS, [1], [done["own"]])
    return influence, done["forward"]


def plain(coupling, diag_inverse, rhs):
    def lower(vector, block):
        return lax.dot_general(
            vector.astype(jnp.bfloat16), block, LOWER, preferred_element_type=jnp.float32
        )

    def upper(vector, block):
        return lax.dot_general(
            vector.astype(jnp.bfloat16), block, UPPER, preferred_element_type=jnp.float32
        )

    solved, answers = {}, {}
    for level in range(LEVELS):
        resid = rhs[level]
        if level:
            terms = [lower(solved[j], coupling[pair_index(level, j)]) for j in range(level)]
            resid = resid - lax.psum(functools.reduce(jnp.add, terms), "rows")
        solved[level] = lax.psum(lower(resid, diag_inverse[level]), "cols")
    for level in range(LEVELS - 1, -1, -1):
        resid = solved[level]
        if level < LEVELS - 1:
            terms = [
                upper(answers[j], coupling[pair_index(j, level)]) for j in range(level + 1, LEVELS)
            ]
            resid = resid - lax.psum(functools.reduce(jnp.add, terms), "cols")
        answers[level] = lax.psum(upper(resid, diag_inverse[level]), "rows")
    stack = lambda found: jnp.stack([found[level] for level in range(LEVELS)])
    return stack(answers), stack(solved)


def body(coupling, diag_inverse, loads, axle_index, *, n_rows, n_cols):
    over_rows, over_cols = diag_inverse.shape[1:]
    if (
        power_of_two(n_rows)
        and power_of_two(n_cols)
        and n_rows > 2
        and n_cols > 1
        and over_cols % (2 * CHUNKS * LANES) == 0
        and over_rows % (2 * LANES) == 0
    ):
        sizes = {"rows": n_rows, "cols": n_cols}
        return staged(coupling, diag_inverse, loads, axle_index, sizes)
    positions = loads.shape[1]
    selector = (axle_index[:, None] == jnp.arange(positions, dtype=jnp.int32)[None, :]).astype(
        jnp.bfloat16
    )
    rhs = jnp.einsum("lp,kpc->klc", selector, loads, preferred_element_type=jnp.float32)
    return plain(coupling, diag_inverse, rhs)


def solution(mesh):
    placed = (
        P("groups", "cols", "rows"),
        P("groups", "rows", "cols"),
        P("groups", None, "cols"),
        P("groups"),
    )
    return jax.shard_map(
        functools.partial(body, n_rows=mesh.shape["rows"], n_cols=mesh.shape["cols"]),
        mesh=mesh,
        in_specs=placed,
        out_specs=(P("groups", None, "cols"), P("groups", None, "rows")),
        check_vma=False,
    )
```

```python
import functools
from typing import NamedTuple

import jax
import jax.numpy as jnp
from jax import lax
from jax.experimental import pallas as pl
from jax.experimental.pallas import tpu as pltpu
from jax.sharding import PartitionSpec as P

LEVELS = 3
COPIES = 8
LANES = 128
CHUNKS = 2
FIRST = 2
IN_VMEM = pl.BlockSpec(memory_space=pltpu.VMEM)
IN_HBM = pl.BlockSpec(memory_space=pltpu.HBM)
SHORT = pl.CostEstimate(flops=0, transcendentals=0, bytes_accessed=0)
LOWER = (((1,), (1,)), ((), ()))
UPPER = (((1,), (0,)), ((), ()))


def pair_index(high, low):
    return high * (high - 1) // 2 + low


def power_of_two(size):
    return size & (size - 1) == 0


class Half(NamedTuple):
    away: int

    def span(self, extent):
        width = self.width(extent)
        at = (lax.axis_index("cols") & 1) ^ self.away
        return pl.ds(pl.multiple_of(at * width, LANES), width)

    def width(self, extent):
        return extent // 2


class Chunk(NamedTuple):
    number: int
    count: int

    def span(self, extent):
        return pl.ds(self.number * (extent - self.width(extent)), self.width(extent))

    def width(self, extent):
        if self.count == 1:
            return extent
        return extent // 2 + (1 * LANES if self.number == 0 else -1 * LANES)


class Job(NamedTuple):
    vectors: list
    places: list
    block: jax.Array
    dims: tuple
    given: list
    outs: list


def in_hbm(blocks):
    return pltpu.with_memory_space_constraint(blocks, pltpu.HBM)


def block_copies(blocks_ref, out_ref, sems, index, pieces):
    height = out_ref.shape[0] // COPIES
    return [
        pltpu.make_async_copy(
            blocks_ref.at[index, pl.ds(i * height, height), :],
            out_ref.at[pl.ds(i * height, height), :],
            sems.at[i],
        )
        for i in pieces
    ]


class Bring(NamedTuple):
    blocks: jax.Array
    index: int
    pieces: range
    held: list


def work(job, bring):
    operands, in_specs, out_shape, scratch, aliases = [], [], [], [], {}
    if job:
        known = [j for j, value in enumerate(job.given) if value is not None]
        operands += [*job.vectors, *(job.given[j] for j in known), job.block]
        in_specs += [IN_VMEM] * len(operands)
        extent = job.block.shape[0 if job.dims is LOWER else 1]
        depth = job.block.shape[1 if job.dims is LOWER else 0]
        rows = job.vectors[0].shape[0]
        out_shape += [
            jax.ShapeDtypeStruct((rows, out.width(extent)), jnp.float32) for out in job.outs
        ]
    if bring:
        aliases = {len(operands): len(out_shape)} if bring.held else {}
        operands += [*bring.held, in_hbm(bring.blocks)]
        in_specs += [IN_VMEM] * len(bring.held) + [IN_HBM]
        out_shape.append(jax.ShapeDtypeStruct(bring.blocks.shape[1:], bring.blocks.dtype))
        scratch.append(pltpu.SemaphoreType.DMA((COPIES,)))

    def kernel(*refs):
        ins, refs = refs[: len(operands)], refs[len(operands) :]
        outs, refs = refs[: len(out_shape)], refs[len(out_shape) :]
        copies = []
        if bring:
            copies = block_copies(ins[-1], outs[-1], refs[0], bring.index, bring.pieces)
        for copy in copies:
            copy.start()
        if job:
            count = len(job.vectors)
            vectors = [ref[...].astype(jnp.bfloat16) for ref in ins[:count]]
            given = dict(zip(known, ins[count:]))
            block_ref = ins[count + len(known)]
            for j, out in enumerate(job.outs):
                total = given[j][...] if j in given else None
                for vector, place in zip(vectors, job.places):
                    inner, outer = place.span(depth), out.span(extent)
                    part = block_ref[outer, inner] if job.dims is LOWER else block_ref[inner, outer]
                    term = lax.dot_general(
                        vector, part, job.dims, preferred_element_type=jnp.float32
                    )
                    total = term if total is None else total + term
                outs[j][...] = total
        for copy in copies:
            copy.wait()

    return pl.pallas_call(
        kernel,
        out_shape=out_shape,
        in_specs=in_specs,
        out_specs=[IN_VMEM] * len(out_shape),
        scratch_shapes=scratch,
        input_output_aliases=aliases,
        compiler_params=pltpu.CompilerParams(vmem_limit_bytes=6 << 20),
        cost_estimate=SHORT,
        name=("products" if job else "fetch") + ("_fetch" if job and bring else ""),
    )(*operands)


def begin(axle_index, loads, blocks, out):
    rows, cols = blocks.shape[1:]
    height = out.width(rows)
    count, positions = axle_index.shape[0], loads.shape[1]
    piece = rows // COPIES
    first = height // piece

    def kernel(index_ref, loads_ref, blocks_ref, *refs):
        selector_ref, vector_ref, part_ref, block_ref, index, table, small_sems, sems = refs
        start = out.span(rows).start
        spans = [
            pl.ds(pl.multiple_of((start + i * piece) % rows, piece), piece) for i in range(COPIES)
        ]
        copies = [
            pltpu.make_async_copy(blocks_ref.at[0, span, :], block_ref.at[span, :], sems.at[i])
            for i, span in enumerate(spans)
        ]
        small = [
            pltpu.make_async_copy(index_ref, index, small_sems.at[0]),
            pltpu.make_async_copy(loads_ref.at[0], table, small_sems.at[1]),
        ]
        for copy in small + copies:
            copy.start()
        for copy in small:
            copy.wait()
        line = lax.broadcasted_iota(jnp.int32, (count, positions), 0)
        wanted = jnp.zeros((count, positions), jnp.int32)
        for i in range(count):
            wanted = jnp.where(line == i, index[i], wanted)
        here = lax.broadcasted_iota(jnp.int32, (count, positions), 1)
        selector = jnp.where(wanted == here, 1.0, 0.0)
        selector_ref[...] = selector
        vector = jnp.dot(
            selector.astype(loads.dtype), table[...], preferred_element_type=jnp.float32
        )
        vector_ref[...] = vector
        for copy in copies[:first]:
            copy.wait()
        part_ref[...] = lax.dot_general(
            vector.astype(blocks.dtype),
            block_ref[pl.ds(pl.multiple_of(start, LANES), height), :],
            LOWER,
            preferred_element_type=jnp.float32,
        )
        for copy in copies[first:]:
            copy.wait()

    return pl.pallas_call(
        kernel,
        out_shape=(
            jax.ShapeDtypeStruct((count, positions), jnp.float32),
            jax.ShapeDtypeStruct((count, cols), jnp.float32),
            jax.ShapeDtypeStruct((count, height), jnp.float32),
            jax.ShapeDtypeStruct((rows, cols), blocks.dtype),
        ),
        in_specs=[IN_HBM] * 3,
        out_specs=[IN_VMEM] * 4,
        scratch_shapes=[
            pltpu.SMEM((count,), jnp.int32),
            pltpu.VMEM((positions, cols), loads.dtype),
            pltpu.SemaphoreType.DMA((2,)),
            pltpu.SemaphoreType.DMA((COPIES,)),
        ],
        compiler_params=pltpu.CompilerParams(vmem_limit_bytes=6 << 20),
        cost_estimate=SHORT,
        name="begin",
    )(in_hbm(axle_index), in_hbm(loads), in_hbm(blocks))


def select(selector, loads, outs):
    found = [(level, out) for level, parts in outs.items() for out in parts]

    def kernel(selector_ref, loads_ref, *out_refs):
        for (level, out), out_ref in zip(found, out_refs):
            out_ref[...] = jnp.dot(
                selector_ref[...].astype(loads.dtype),
                loads_ref[level, :, out.span(loads.shape[2])],
                preferred_element_type=jnp.float32,
            )

    result = pl.pallas_call(
        kernel,
        out_shape=[
            jax.ShapeDtypeStruct((selector.shape[0], out.width(loads.shape[2])), jnp.float32)
            for _, out in found
        ],
        in_specs=[IN_VMEM, IN_VMEM],
        out_specs=[IN_VMEM] * len(found),
        compiler_params=pltpu.CompilerParams(vmem_limit_bytes=6 << 20),
        cost_estimate=SHORT,
        name="select",
    )(selector, loads)
    return {key: [r for (level, _), r in zip(found, result) if level == key] for key in outs}


def place(pieces, targets, width, held):
    rows = pieces[0].shape[0]

    def kernel(*refs):
        out_ref, sems = refs[-2:]
        copies = [
            pltpu.make_async_copy(ref, out_ref.at[level, :, part.span(width)], sems.at[i])
            for i, (ref, (level, part)) in enumerate(zip(refs, targets))
        ]
        for copy in copies:
            copy.start()
        for copy in copies:
            copy.wait()

    return pl.pallas_call(
        kernel,
        out_shape=jax.ShapeDtypeStruct((LEVELS, rows, width), jnp.float32),
        in_specs=[IN_VMEM] * len(pieces) + [IN_HBM] * len(held),
        out_specs=IN_HBM,
        scratch_shapes=[pltpu.SemaphoreType.DMA((len(pieces),))],
        input_output_aliases={len(pieces): 0} if held else {},
        compiler_params=pltpu.CompilerParams(vmem_limit_bytes=6 << 20),
        cost_estimate=SHORT,
        name="place",
    )(*pieces, *held)


class Order:
    def __init__(self):
        self.last = ()

    def after(self, *values):
        *values, self.last = lax.optimization_barrier((*values, self.last))
        return values

    def run(self, function, *values):
        self.last = function(*self.after(*values))
        return self.last


def staged(coupling, diag_inverse, loads, axle_index, sizes):
    order = Order()
    blocks = {}
    def steps(axis, col=0):
        found = [1 << i for i in range(sizes[axis].bit_length() - 1)]
        if axis == "rows" and col % 2:
            found[:2] = [3, 1]
        return found

    own, away = Half(0), Half(1)

    def pieces_of(count):
        return [Chunk(number, count) for number in range(count)]

    def taking(bring):
        if not bring:
            return []
        return [blocks[bring[0]]] if bring[0] in blocks else []

    def source(bring, held):
        if not bring:
            return None
        (kind, index), pieces = bring
        return Bring(diag_inverse if kind == "diag" else coupling, index, pieces, held)

    def products(vectors, places, name, dims, given, outs, bring=None):
        count = len(vectors)
        known = [value for value in given or () if value is not None]
        held = taking(bring)

        def call(*values):
            left = iter(values[count + 1 :])
            terms = [None if value is None else next(left) for value in given or ()]
            job = Job(values[:count], places, values[count], dims, terms, outs)
            return work(job, source(bring, list(left)))

        result = list(order.run(call, *vectors, blocks[name], *known, *held))
        if bring:
            blocks[bring[0]] = result.pop()
        return result

    def fetch(name, pieces=range(COPIES)):
        def call():
            bring = name, pieces
            held = taking(bring)
            (blocks[name],) = order.run(lambda *found: work(None, source(bring, list(found))), *held)

        return call

    def permute(value, axis, number):
        (value,) = order.after(value)
        if axis == "cols":
            step = steps(axis)[number]
            return lax.ppermute(value, axis, [(i, i ^ step) for i in range(sizes[axis])])
        n_cols = sizes["cols"]
        moves = [
            (row * n_cols + col, (row ^ steps(axis, col)[number]) * n_cols + col)
            for row in range(sizes[axis])
            for col in range(n_cols)
        ]
        return lax.ppermute(value, ("rows", "cols"), moves)

    def nothing():
        pass

    def settle(found):
        value, place = found[-1]
        if callable(value):
            found[-1] = value(), place
        return found

    def onto(found, onward, late=nothing):
        name, dims, outs, given = onward
        given = given and given()
        if given:
            given = given + [None] * (len(outs) - len(given))
        for vector, place in found[:-1]:
            (vector,) = order.after(vector)
            given = products([vector], [place], name, dims, given, outs)
            late()
            late = nothing
        late()
        settle(found)
        (vector,), (place,) = order.after(found[-1][0]), found[-1][1:]

        def finish(which, bring=None):
            terms = given and [given[i] for i in which]
            return products([vector], [place], name, dims, terms, [outs[i] for i in which], bring)

        return finish

    def cols_sum(finish, middle=nothing, post=None):
        got = permute(finish([0])[0], "cols", 0)
        (kept,) = finish([1])
        last = len(steps("cols"))
        for number in range(1, last + 1):
            kept = order.run(jnp.add, kept, got)
            if number == last and post is not None:
                kept = order.run(jnp.subtract, post(), kept)
            got = permute(kept, "cols", number % last)
            if number < last:
                middle()
                middle = nothing
        return [(kept, own), (got, away)]

    def rows_sum(finish, count, early=nothing, middle=nothing, post=None, during=None):
        every = range(count)
        kept, got = [], []
        for i in every:
            kept += finish([i], during if i == count - 1 else None)
            got.append(permute(kept[i], "rows", 0))
        more = early()
        last = len(steps("rows"))
        for number in range(1, last + 1):
            for i in every[:-1] if number == last else every:
                if more and number == 1:
                    kept[i] = order.run(jnp.add, kept[i], more[i])
                kept[i] = order.run(jnp.add, kept[i], got[i])
                if number < last:
                    got[i] = permute(kept[i], "rows", number)
                elif post is not None:
                    kept[i] = order.run(jnp.subtract, post()[i], kept[i])
            if number < last:
                middle()
                middle = nothing

        def rest():
            value = order.run(jnp.add, kept[-1], got[-1])
            return value if post is None else order.run(jnp.subtract, post()[-1], value)

        return list(zip(kept[:-1] + [rest], pieces_of(count)))

    def pair(high, low):
        return "coupling", pair_index(high, low)

    chunks = {level: FIRST if level == 1 else CHUNKS for level in range(1, LEVELS)}
    selector, vector, first, blocks["diag", 0] = order.run(
        lambda: begin(axle_index, loads, diag_inverse, away)
    )
    rhs, solved, answers, skipped, done = {}, {}, {}, {}, {}

    def first_finish(which):
        if which == [0]:
            return [first]
        return products([vector], pieces_of(1), ("diag", 0), LOWER, None, [own])

    def prepare():
        del blocks["diag", 0]
        wanted = {level: pieces_of(count) for level, count in chunks.items()}
        rhs.update(order.run(lambda a, b: select(a, b, wanted), selector, loads))
        fetch(pair(1, 0))()

    def skip(found, dims, outs):
        vectors, places = zip(*found)
        skipped[dims] = products(list(vectors), list(places), pair(2, 0), dims, None, outs)

    def skip_forward():
        skip(solved[0], LOWER, pieces_of(chunks[2]))

    def skip_backward():
        skip(answers[2], UPPER, [away, own])

    def put(found, levels, width, held=()):
        flat = [(value, (level, part)) for level in levels for value, part in found[level]]
        values, targets = zip(*flat)
        number = len(values)
        return order.run(
            lambda *values: place(values[:number], targets, width, values[number:]), *values, *held
        )

    def put_forward():
        done["forward"] = put(solved, range(LEVELS), diag_inverse.shape[1])

    def put_early():
        done["early"] = put(answers, [2, 1], diag_inverse.shape[2])

    halves = [away, own]
    solved[0] = cols_sum(first_finish, prepare)
    finish = onto(solved[0], (pair(1, 0), LOWER, pieces_of(chunks[1]), None))
    whole = range(COPIES)
    found = rows_sum(
        finish, chunks[1], nothing, fetch(pair(2, 0)), lambda: rhs[1], (("diag", 1), whole)
    )
    finish = onto(found, (("diag", 1), LOWER, halves, None), skip_forward)
    solved[1] = cols_sum(finish, fetch(pair(2, 1)))
    finish = onto(solved[1], (pair(2, 1), LOWER, pieces_of(chunks[2]), lambda: skipped[LOWER]))
    found = rows_sum(finish, chunks[2], nothing, fetch(("diag", 2)), lambda: rhs[2])
    finish = onto(found, (("diag", 2), LOWER, halves, None))
    solved[2] = cols_sum(finish)
    finish = onto(solved[2], (("diag", 2), UPPER, pieces_of(CHUNKS), None))
    answers[2] = rows_sum(finish, CHUNKS)
    finish = onto(answers[2], (pair(2, 1), UPPER, halves, None))
    found = cols_sum(finish, skip_backward, lambda: solved[1][0][0])
    finish = onto(found, (("diag", 1), UPPER, pieces_of(CHUNKS), None))
    answers[1] = rows_sum(finish, CHUNKS, middle=fetch(("diag", 0)))
    finish = onto(answers[1], (pair(1, 0), UPPER, halves, lambda: skipped[UPPER]))
    found = cols_sum(finish, put_forward, lambda: solved[0][0][0])
    finish = onto(found, (("diag", 0), UPPER, pieces_of(CHUNKS), None))
    answers[0] = settle(rows_sum(finish, CHUNKS, middle=put_early))
    influence = put(answers, [0], diag_inverse.shape[2], [done["early"]])
    return influence, done["forward"]


def plain(coupling, diag_inverse, rhs):
    def lower(vector, block):
        return lax.dot_general(
            vector.astype(jnp.bfloat16), block, LOWER, preferred_element_type=jnp.float32
        )

    def upper(vector, block):
        return lax.dot_general(
            vector.astype(jnp.bfloat16), block, UPPER, preferred_element_type=jnp.float32
        )

    solved, answers = {}, {}
    for level in range(LEVELS):
        resid = rhs[level]
        if level:
            terms = [lower(solved[j], coupling[pair_index(level, j)]) for j in range(level)]
            resid = resid - lax.psum(functools.reduce(jnp.add, terms), "rows")
        solved[level] = lax.psum(lower(resid, diag_inverse[level]), "cols")
    for level in range(LEVELS - 1, -1, -1):
        resid = solved[level]
        if level < LEVELS - 1:
            terms = [
                upper(answers[j], coupling[pair_index(j, level)]) for j in range(level + 1, LEVELS)
            ]
            resid = resid - lax.psum(functools.reduce(jnp.add, terms), "cols")
        answers[level] = lax.psum(upper(resid, diag_inverse[level]), "rows")
    stack = lambda found: jnp.stack([found[level] for level in range(LEVELS)])
    return stack(answers), stack(solved)


def body(coupling, diag_inverse, loads, axle_index, *, n_rows, n_cols):
    over_rows, over_cols = diag_inverse.shape[1:]
    if (
        power_of_two(n_rows)
        and power_of_two(n_cols)
        and n_rows > 2
        and n_cols > 1
        and over_cols % (2 * CHUNKS * LANES) == 0
        and over_rows % (2 * LANES) == 0
    ):
        sizes = {"rows": n_rows, "cols": n_cols}
        return staged(coupling, diag_inverse, loads, axle_index, sizes)
    positions = loads.shape[1]
    selector = (axle_index[:, None] == jnp.arange(positions, dtype=jnp.int32)[None, :]).astype(
        jnp.bfloat16
    )
    rhs = jnp.einsum("lp,kpc->klc", selector, loads, preferred_element_type=jnp.float32)
    return plain(coupling, diag_inverse, rhs)


def solution(mesh):
    placed = (
        P("groups", "cols", "rows"),
        P("groups", "rows", "cols"),
        P("groups", None, "cols"),
        P("groups"),
    )
    return jax.shard_map(
        functools.partial(body, n_rows=mesh.shape["rows"], n_cols=mesh.shape["cols"]),
        mesh=mesh,
        in_specs=placed,
        out_specs=(P("groups", None, "cols"), P("groups", None, "rows")),
        check_vma=False,
    )
```
